256 devices in a mesh: day: 4 (over x), sta: 64 (over y, z, core).
Axes of the slice: x: 4, y: 4, z: 8, core: 2. Of those that a mesh axis runs over, the one named last changes fastest.
Arguments:
- raw_spectra: bfloat16 [96, 8192, 2, 128], P('day', 'sta'), may hold values from -6 to 6
- station_block: int32 [8192], replicated, may hold values from 0 to 63, as said below
- pair_listed: int32 [64, 3], P('sta'), may hold values 0 or 1
Outputs:
- stacks: bfloat16 [64, 3, 2, 128, 128, 128], P('sta', None, None, 'day')
The draws below stay inside these ranges and needn't reach their ends.
Inputs may be any that keep to these rules, and one draw needn't show every extreme that they name: `station_block`: every block holds exactly 128 stations; of the 128 consecutive stations of one ingest shard at most 3 belong to one block, and every shard reaches that most.
All inputs are finite; a program needn't handle non-finite values. No bound on the sum of `pair_listed` on one device may be relied on, other than what follows from the above.
Results may differ from the reference program's by a relative error of at most 0.012.
Values may be sent and summed in bfloat16 or wider, within the bound.
A program may use at most 128 MiB of HBM per device.

```python
import jax
import jax.numpy as jnp
from jax import lax

BLOCK = 128
FB = 128
SEG_DEV = 24
WIN = 3
STATIONS = 8192
SEGS = 96
N_DAY = 4
N_STA = 64


def draw_station_block(key, part):
    blocks = STATIONS // BLOCK
    base = BLOCK // blocks
    first_key, second_key = jax.random.split(jax.random.fold_in(key, 17))
    mapping = jax.random.permutation(first_key, blocks).astype(jnp.int32)
    shards = jnp.arange(blocks, dtype=jnp.int32)
    counts = jnp.full((blocks, blocks), base, jnp.int32)
    counts = counts.at[shards, mapping].add(1)
    counts = counts.at[shards, (mapping + 1) % blocks].add(-1)
    bounds = jnp.cumsum(counts, axis=1)
    slots = jnp.arange(BLOCK, dtype=jnp.int32)
    labels = jnp.sum((bounds[:, None, :] <= slots[None, :, None]).astype(jnp.int32), axis=2)
    shard_keys = jax.random.split(second_key, blocks)
    shuffled = jax.vmap(lambda one_key, row: jax.random.permutation(one_key, row))(shard_keys, labels)
    return shuffled.reshape(-1).astype(jnp.int32)


def plant(entries, stream_key, smallest, high):
    longest = entries.shape.index(max(entries.shape))
    spots = []
    for shift in (0, 1):
        where = [jax.random.randint(jax.random.fold_in(stream_key, axis), (), 0, length) for axis, length in enumerate(entries.shape)]
        where[longest] = (where[longest] + shift) % entries.shape[longest]
        spots.append(tuple(where))
    return entries.at[spots[0]].set(smallest).at[spots[1]].set(high)


def levels(stream_key, shape, cuts, least, top_value):
    factor_of = 1.0
    for position, shards_of in cuts:
        draws = jax.random.uniform(jax.random.fold_in(jax.random.fold_in(stream_key, 6), position), (shards_of,), jnp.float32, least / len(cuts), top_value / len(cuts))
        factor_of = factor_of * jnp.repeat(jnp.exp(draws), shape[position] // shards_of).reshape((-1,) + (1,) * (len(shape) - 1 - position))
    return factor_of


def gaussian(rng, dims, deviation, most, cuts=(), held_as=jnp.bfloat16):
    gain = levels(rng, dims, cuts, -0.22, 0.18) if cuts else 1.0
    array = jax.random.normal(rng, dims, jnp.float32) * deviation * gain
    return jnp.minimum(jnp.maximum(array, -most), most).astype(held_as)


def setup_inputs(seed: int = 0) -> dict:
    key_of = jax.random.split(jax.random.key(seed), 4)
    raw_spectra = gaussian(key_of[0], (SEGS, STATIONS, 2, FB), 1.0, 6.0, ((0, 4), (1, 64)))
    station_block = draw_station_block(jax.random.fold_in(key_of[3], 71), 0)
    pair_listed = plant((jax.random.randint(key_of[2], (N_STA, WIN), 0, 4) < 3).astype(jnp.int32), jax.random.fold_in(key_of[2], 1), 0, 1)
    return dict(raw_spectra=raw_spectra, station_block=station_block, pair_listed=pair_listed)


def whiten(raw_spectra):
    values = raw_spectra.astype(jnp.float32)
    power = values[:, :, 0, :] ** 2 + values[:, :, 1, :] ** 2
    level = lax.optimization_barrier(jnp.mean(power, axis=-1, keepdims=True))
    scaled = values / jnp.sqrt(power + level + 1e-05)[:, :, None, :]
    return scaled.astype(jnp.bfloat16)

def correlate(first, second):
    first = first.astype(jnp.float32)
    second = second.astype(jnp.float32)
    real_a = first[:, :, :, 0, :]
    imag_a = first[:, :, :, 1, :]
    real_b = second[:, :, :, 0, :]
    imag_b = second[:, :, :, 1, :]
    real_part = jnp.einsum('gsif,gsjf->gfij', real_a, real_b) + jnp.einsum('gsif,gsjf->gfij', imag_a, imag_b)
    imag_part = jnp.einsum('gsif,gsjf->gfij', real_a, imag_b) - jnp.einsum('gsif,gsjf->gfij', imag_a, real_b)
    return jnp.stack([real_part, imag_part], axis=1)

def reference(raw_spectra, station_block, pair_listed):
    white = whiten(raw_spectra)
    order = jnp.argsort(station_block, stable=True)
    blocked = white[:, order].reshape(N_DAY, SEG_DEV, N_STA, BLOCK, 2, FB)
    scale = 1.0 / jnp.sqrt(jnp.float32(SEGS))

    def one_row(row):
        first = lax.dynamic_index_in_dim(blocked, row, 2, keepdims=False)
        results = []
        for offset in range(WIN):
            column = ((row + offset) % N_STA).astype(jnp.int32)
            second = lax.dynamic_index_in_dim(blocked, column, 2, keepdims=False)
            parts = correlate(first, second).astype(jnp.bfloat16)
            parts = lax.optimization_barrier(parts).astype(jnp.float32)
            total = lax.optimization_barrier(jnp.sum(parts, axis=0))
            weight = pair_listed[row, offset].astype(jnp.float32)
            results.append(total * weight * scale)
        return jnp.stack(results).astype(jnp.bfloat16)
    return lax.map(one_row, jnp.arange(N_STA, dtype=jnp.int32))
```

```python
import jax
import jax.numpy as jnp
from jax import lax
from jax.sharding import PartitionSpec as P


def shifted(block, axis, distance):
    devices = range(lax.axis_size(axis))
    route = [((i - distance) % len(devices), i) for i in devices]
    return lax.ppermute(block, axis, route)


def correlate(first, second):
    swapped = jnp.stack([second[:, :, 1], -second[:, :, 0]], axis=2)
    paired = jnp.stack([second, swapped], axis=3)
    return jnp.einsum("iscf,jscpf->pfij", first, paired, preferred_element_type=jnp.float32)


def local(raw_spectra, station_block, pair_listed):
    blocks = lax.axis_size("sta")
    groups = lax.axis_size("day")
    me_block = lax.axis_index("sta")
    segments, block_size, _, bins = raw_spectra.shape
    window = pair_listed.shape[1]
    most = 3
    share = bins // groups
    rows = segments * 2 * share // 128
    values = raw_spectra.astype(jnp.float32)
    power = values[:, :, 0, :] ** 2 + values[:, :, 1, :] ** 2
    level = jnp.mean(power, axis=-1, keepdims=True)
    white = (values / jnp.sqrt(power + level + 1e-05)[:, :, None, :]).astype(jnp.bfloat16)
    by_owner = jnp.transpose(white.reshape(segments, block_size, 2, groups, share), (3, 1, 0, 2, 4))
    by_owner = by_owner.reshape(groups, block_size, rows, 128)
    by_day = lax.all_to_all(by_owner, "day", split_axis=0, concat_axis=0, tiled=True)
    by_station = jnp.transpose(by_day, (1, 0, 2, 3)).reshape(block_size, groups * rows, 128)
    labels = jnp.arange(blocks, dtype=jnp.int32)
    full_hot = (station_block[:, None] == labels[None, :]).astype(jnp.int32)
    counts = jnp.sum(full_hot.reshape(blocks, block_size, blocks), axis=1)
    before = (labels[:, None] < labels[None, :]).astype(jnp.int32)
    earlier = jnp.sum(before[:, :, None] * counts[:, None, :], axis=0)
    own_blocks = lax.dynamic_slice_in_dim(station_block, me_block * block_size, block_size)
    own_hot = (own_blocks[:, None] == labels[None, :]).astype(jnp.int32)
    rank_in = jnp.sum((jnp.cumsum(own_hot, axis=0) - own_hot) * own_hot, axis=1)
    outgoing = jnp.zeros((blocks, most, groups * rows, 128), jnp.bfloat16)
    outgoing = outgoing.at[own_blocks, rank_in].set(by_station)
    incoming = lax.all_to_all(outgoing, "sta", split_axis=0, concat_axis=0, tiled=True)
    source_counts = lax.dynamic_slice_in_dim(counts, me_block, 1, axis=1)
    source_start = lax.dynamic_slice_in_dim(earlier, me_block, 1, axis=1)
    slot_rank = jnp.arange(most, dtype=jnp.int32)[None, :]
    target = jnp.where(slot_rank < source_counts, source_start + slot_rank, block_size).reshape(-1)
    arranged = jnp.zeros((block_size, groups * rows, 128), jnp.bfloat16)
    arranged = arranged.at[target].set(incoming.reshape(blocks * most, groups * rows, 128), mode="drop")
    scale = 1.0 / jnp.sqrt(jnp.float32(segments * groups))
    weights = pair_listed[0].astype(jnp.float32)
    fields = [arranged] + [shifted(arranged, "sta", -offset) for offset in range(1, window)]
    fields = [f.reshape(block_size, groups * segments, 2, share) for f in fields]
    results = []
    for offset in range(window):
        product = correlate(fields[0], fields[offset])
        results.append((product * (weights[offset] * scale)).astype(jnp.bfloat16))
    return jnp.stack(results)[None]


def solution(mesh):
    in_specs = (P("day", "sta", None, None), P(), P("sta", None))
    out_specs = P("sta", None, None, "day", None, None)
    return jax.shard_map(local, mesh=mesh, in_specs=in_specs, out_specs=out_specs, check_vma=False)
```

```python
import functools

import jax
import jax.numpy as jnp
from jax import lax
from jax.experimental import pallas as pl
from jax.experimental.pallas import tpu as pltpu
from jax.sharding import PartitionSpec as P

MOST = 3
LANES = 128
MESH = pl.DeviceIdType.MESH
BF16 = jnp.bfloat16
F32 = jnp.float32


def iota(shape, axis):
    return lax.broadcasted_iota(jnp.int32, shape, axis)


def whiten_kernel(me, quads, raw_ref, table_ref, out_ref, pick_ref):
    rows = raw_ref.shape[1]
    slots = out_ref.shape[2]
    stations = rows // 2

    @pl.when(pl.program_id(0) == 0)
    def _():
        own = table_ref[pl.ds(me(), 1), :]
        across = jnp.broadcast_to(own, (stations, stations))
        down = jnp.transpose(across)
        same = (across == down) & (iota((stations, stations), 0) < iota((stations, stations), 1))
        rank = jnp.sum(same.astype(F32), axis=0, keepdims=True)
        slot = own.astype(F32) * MOST + rank
        spread = (lax.shift_right_logical(iota((stations, rows), 1), 1) == iota((stations, rows), 0)).astype(BF16)
        slot = jnp.broadcast_to(slot, (8, stations)).astype(BF16)
        wide = jnp.dot(slot, spread, preferred_element_type=F32)[0:1].astype(jnp.int32)
        place = wide * 2 + (iota((1, rows), 1) & 1)
        pick_ref[...] = (iota((slots, rows), 0) == place).astype(F32).astype(BF16)

    lane = iota((rows, LANES), 1)
    low = lane < 64
    even = (lane & 32) == 0
    odd_row = (iota((rows // 8, 8, LANES), 1) & 1) == 1
    pick = pick_ref[...]
    for quad in range(quads):
        white = []
        for part in range(4):
            x = raw_ref[quad * 4 + part].astype(F32)
            square = (x * x).reshape(rows // 8, 8, LANES)
            other = jnp.where(odd_row, pltpu.roll(square, 1, 1), pltpu.roll(square, 7, 1))
            power = (square + other).reshape(rows, LANES)
            level = jnp.sum(power, axis=1, keepdims=True) * (1.0 / LANES)
            white.append(x * lax.rsqrt(power + level + 1e-05))
        w0, w1, w2, w3 = white
        a0 = jnp.where(low, w0, pltpu.roll(w2, 64, 1))
        a2 = jnp.where(low, pltpu.roll(w0, 64, 1), w2)
        a1 = jnp.where(low, w1, pltpu.roll(w3, 64, 1))
        a3 = jnp.where(low, pltpu.roll(w1, 64, 1), w3)
        d0 = jnp.where(even, a0, pltpu.roll(a1, 32, 1))
        d1 = jnp.where(even, pltpu.roll(a0, 96, 1), a1)
        d2 = jnp.where(even, a2, pltpu.roll(a3, 32, 1))
        d3 = jnp.where(even, pltpu.roll(a2, 96, 1), a3)
        for half, (first, second) in enumerate(((d0, d1), (d2, d3))):
            both = jnp.concatenate([first.astype(BF16), second.astype(BF16)], axis=1)
            sent = jnp.dot(pick, both, preferred_element_type=F32).astype(BF16)
            out_ref[2 * half, quad] = sent[:, :LANES]
            out_ref[2 * half + 1, quad] = sent[:, LANES:]


def whiten(raw, table, me):
    segments, rows, _ = raw.shape
    quads = segments // 4
    step = 3
    slots = table.shape[0] * MOST * 2
    return pl.pallas_call(
        functools.partial(whiten_kernel, me, step),
        out_shape=jax.ShapeDtypeStruct((4, quads, slots, LANES), BF16),
        grid=(quads // step,),
        in_specs=[
            pl.BlockSpec((4 * step, rows, LANES), lambda i: (i, 0, 0)),
            pl.BlockSpec(table.shape, lambda i: (0, 0)),
        ],
        out_specs=pl.BlockSpec((4, step, slots, LANES), lambda i: (0, i, 0, 0)),
        scratch_shapes=[pltpu.VMEM((slots, rows), BF16)],
        name="whiten",
    )(raw, table)


def exchange_kernel(days, blocks, send, recv, send_sem, recv_sem):
    g = lax.axis_index("day")
    s = lax.axis_index("sta")
    own = pltpu.make_async_copy(send.at[g, :, s], recv.at[g, :, s], recv_sem.at[0])
    own.start()

    def start(d, b, kind):
        pltpu.make_async_remote_copy(
            src_ref=send.at[d, :, b],
            dst_ref=recv.at[g, :, s],
            send_sem=send_sem.at[kind],
            recv_sem=recv_sem.at[kind],
            device_id=(d, b),
            device_id_type=MESH,
        ).start()

    for turn in range(1, days):
        start(lax.rem(g + turn, days), s, 1)

    def step(t, carry):
        b = lax.rem(s + t, blocks)
        start(g, b, 0)
        for turn in range(1, days):
            start(lax.rem(g + turn, days), b, 1)
        return carry

    lax.fori_loop(1, blocks, step, 0)
    few = send.at[0, :, pl.ds(0, blocks - 1)]
    pltpu.make_async_copy(few, few, send_sem.at[0]).wait()
    rest = send.at[pl.ds(0, days - 1)]
    pltpu.make_async_copy(rest, rest, send_sem.at[1]).wait()
    pltpu.make_async_copy(recv.at[0], recv.at[0], recv_sem.at[0]).wait()
    rest = recv.at[pl.ds(0, days - 1)]
    pltpu.make_async_copy(rest, rest, recv_sem.at[1]).wait()


def exchange(send):
    days, _, blocks = send.shape[:3]
    return pl.pallas_call(
        functools.partial(exchange_kernel, days, blocks),
        out_shape=jax.ShapeDtypeStruct(send.shape, send.dtype),
        in_specs=[pl.BlockSpec(memory_space=pl.ANY)],
        out_specs=pl.BlockSpec(memory_space=pl.ANY),
        scratch_shapes=[pltpu.SemaphoreType.DMA((2,)), pltpu.SemaphoreType.DMA((2,))],
        compiler_params=pltpu.CompilerParams(has_side_effects=True),
        name="exchange",
    )(send)


def arrange_kernel(me, quads, recv_ref, table_ref, out_ref, pick_ref, wide_ref):
    slots = recv_ref.shape[1]
    shards, stations = table_ref.shape
    bins, depth, _ = out_ref.shape
    count = depth // 2

    @pl.when(pl.program_id(0) == 0)
    def _():
        mine = jnp.sum((table_ref[...] == me()).astype(F32), axis=1, keepdims=True)
        mine = jnp.broadcast_to(mine, (shards, LANES)).astype(BF16)
        lower = (iota((shards, shards), 1) < iota((shards, shards), 0)).astype(F32).astype(BF16)
        first = jnp.dot(lower, mine, preferred_element_type=F32)
        shard = iota((slots, shards), 1)
        row = iota((slots, shards), 0)
        member = ((row >= 6 * shard) & (row < 6 * shard + 6)).astype(F32).astype(BF16)
        first = jnp.dot(member, first.astype(BF16), preferred_element_type=F32).astype(jnp.int32)
        mine = jnp.dot(member, mine, preferred_element_type=F32).astype(jnp.int32)
        index = iota((shards, LANES), 0).astype(F32).astype(BF16)
        index = jnp.dot(member, index, preferred_element_type=F32).astype(jnp.int32)
        rest = iota((slots, LANES), 0) - 6 * index
        rank = lax.shift_right_logical(rest, 1)
        hit = (rank < mine) & (first + rank == iota((slots, LANES), 1))
        for part in range(2):
            chosen = (hit & ((rest & 1) == part)).astype(F32).astype(BF16)
            pick_ref[:, part * LANES:(part + 1) * LANES] = chosen

    pick = pick_ref[...]
    base = pl.program_id(0) * (4 * quads)
    for quad in range(quads):
        block = lax.dot_general(recv_ref[quad], pick, (((0,), (0,)), ((), ())), preferred_element_type=F32)
        for part in range(4):
            for kind in range(2):
                where = pl.ds(kind * count + base + quad * 4 + part, bins, stride=depth)
                wide_ref[where, :] = block[part * bins:(part + 1) * bins, kind * LANES:(kind + 1) * LANES]

    @pl.when(pl.program_id(0) == pl.num_programs(0) - 1)
    def _():
        def step(f, carry):
            out_ref[f] = wide_ref[pl.ds(pl.multiple_of(f * depth, depth), depth), :].astype(BF16)
            return carry

        lax.fori_loop(0, bins, step, 0)


def arrange(recv, table, me):
    total, slots, _ = recv.shape
    steps = 4
    quads = total // steps
    bins = LANES // 4
    depth = 2 * 4 * total
    return pl.pallas_call(
        functools.partial(arrange_kernel, me, quads),
        out_shape=jax.ShapeDtypeStruct((bins, depth, LANES), BF16),
        grid=(steps,),
        in_specs=[
            pl.BlockSpec((quads, slots, LANES), lambda i: (i, 0, 0)),
            pl.BlockSpec(table.shape, lambda i: (0, 0)),
        ],
        out_specs=pl.BlockSpec((bins, depth, LANES), lambda i: (0, 0, 0)),
        scratch_shapes=[pltpu.VMEM((slots, 2 * LANES), BF16), pltpu.VMEM((bins * depth, LANES), F32)],
        name="arrange",
    )(recv, table)


def neighbour_kernel(blocks, chunks, own, near, send_far, recv_far, send_near, recv_near):
    s = lax.axis_index("sta")
    g = lax.axis_index("day")
    odd = lax.rem(s, 2)
    partner = s + 1 - 2 * odd
    before = lax.rem(s + blocks - 2, blocks)
    after = lax.rem(s + 2, blocks)
    size = own.shape[0] // chunks

    barrier = pltpu.get_barrier_semaphore()
    for peer in (after, partner):
        pl.semaphore_signal(barrier, inc=1, device_id=(g, peer), device_id_type=MESH)
    pl.semaphore_wait(barrier, 2)

    def far(i):
        part = pl.ds(i * size, size)
        return pltpu.make_async_remote_copy(
            src_ref=own.at[part], dst_ref=near.at[1, part], send_sem=send_far.at[i], recv_sem=recv_far.at[i],
            device_id=(g, before), device_id_type=MESH)

    def close(i, source):
        part = pl.ds(i * size, size)
        return pltpu.make_async_remote_copy(
            src_ref=source.at[part], dst_ref=near.at[0, part], send_sem=send_near.at[i], recv_sem=recv_near.at[i],
            device_id=(g, partner), device_id_type=MESH)

    for i in range(chunks):
        far(i).start()

    @pl.when(odd == 1)
    def _():
        for i in range(chunks):
            close(i, own).start()
        for i in range(chunks):
            far(i).wait_recv()

    @pl.when(odd == 0)
    def _():
        for i in range(chunks):
            far(i).wait_recv()
            close(i, near.at[1]).start()

    for i in range(chunks):
        close(i, own).wait_recv()
    for i in range(chunks):
        close(i, own).wait_send()
        far(i).wait_send()


def neighbours(own, blocks):
    chunks = 8
    return pl.pallas_call(
        functools.partial(neighbour_kernel, blocks, chunks),
        out_shape=jax.ShapeDtypeStruct((2,) + own.shape, own.dtype),
        in_specs=[pl.BlockSpec(memory_space=pl.ANY)],
        out_specs=pl.BlockSpec(memory_space=pl.ANY),
        scratch_shapes=[pltpu.SemaphoreType.DMA((chunks,))] * 4,
        compiler_params=pltpu.CompilerParams(collective_id=1, has_side_effects=True),
        name="neighbours",
    )(own)


def correlate_kernel(scale, listed_ref, own_ref, near_ref, out_ref):
    bins, depth, width = own_ref.shape
    half = depth // 2
    gains = [listed_ref[0, o].astype(F32) * scale for o in range(3)]

    def one(f):
        own = own_ref[f]
        real, imag = own[:half], own[half:]
        left = jnp.concatenate(
            [jnp.concatenate([real, -imag], axis=1), jnp.concatenate([imag, real], axis=1)], axis=0)
        right = jnp.concatenate([own, near_ref[0, f], near_ref[1, f]], axis=1)
        product = lax.dot_general(left, right, (((0,), (0,)), ((), ())), preferred_element_type=F32)
        for o in range(3):
            for part in range(2):
                piece = product[part * width:(part + 1) * width, o * width:(o + 1) * width]
                out_ref[0, o, part, f] = (piece * gains[o]).astype(BF16)

    for f in range(bins):
        one(f)


def stack(own, near, listed, scale):
    bins, depth, width = own.shape
    step = 4
    return pl.pallas_call(
        functools.partial(correlate_kernel, scale),
        out_shape=jax.ShapeDtypeStruct((1, 3, 2, bins, width, width), BF16),
        grid=(bins // step,),
        in_specs=[
            pl.BlockSpec(memory_space=pltpu.SMEM),
            pl.BlockSpec((step, depth, width), lambda i: (i, 0, 0)),
            pl.BlockSpec((2, step, depth, width), lambda i: (0, i, 0, 0)),
        ],
        out_specs=pl.BlockSpec((1, 3, 2, step, width, width), lambda i: (0, 0, 0, i, 0, 0)),
        name="stack",
    )(listed, own, near)


def local(raw_spectra, station_block, pair_listed):
    blocks = lax.axis_size("sta")
    days = lax.axis_size("day")
    segments, stations, _, bins = raw_spectra.shape
    quads = segments // 4
    me = lambda: lax.axis_index("sta")
    table = station_block.reshape(blocks, stations)
    sent = whiten(raw_spectra.reshape(segments, 2 * stations, bins), table, me)
    got = exchange(sent.reshape(days, quads, blocks, MOST, 2, LANES))
    own = arrange(got.reshape(days * quads, blocks * MOST * 2, LANES), table, me)
    near = neighbours(own, blocks)
    scale = 1.0 / float(segments * days) ** 0.5
    return stack(own, near, pair_listed, scale)


def solution(mesh):
    in_specs = (P("day", "sta", None, None), P(), P("sta", None))
    out_specs = P("sta", None, None, "day", None, None)
    return jax.shard_map(local, mesh=mesh, in_specs=in_specs, out_specs=out_specs, check_vma=False)
```

```python
import functools

import jax
import jax.numpy as jnp
from jax import lax
from jax.experimental import pallas as pl
from jax.experimental.pallas import tpu as pltpu
from jax.sharding import PartitionSpec as P

MOST = 3
LANES = 128
MESH = pl.DeviceIdType.MESH
BF16 = jnp.bfloat16
F32 = jnp.float32


def iota(shape, axis):
    return lax.broadcasted_iota(jnp.int32, shape, axis)


def whiten_kernel(me, quads, raw_ref, table_ref, out_ref, pick_ref):
    rows = raw_ref.shape[1]
    slots = out_ref.shape[2]
    stations = rows // 2

    @pl.when(pl.program_id(0) == 0)
    def _():
        own = table_ref[pl.ds(me(), 1), :]
        across = jnp.broadcast_to(own, (stations, stations))
        down = jnp.transpose(across)
        same = (across == down) & (iota((stations, stations), 0) < iota((stations, stations), 1))
        rank = jnp.sum(same.astype(F32), axis=0, keepdims=True)
        slot = own.astype(F32) * MOST + rank
        spread = (lax.shift_right_logical(iota((stations, rows), 1), 1) == iota((stations, rows), 0)).astype(BF16)
        slot = jnp.broadcast_to(slot, (8, stations)).astype(BF16)
        wide = jnp.dot(slot, spread, preferred_element_type=F32)[0:1].astype(jnp.int32)
        place = wide * 2 + (iota((1, rows), 1) & 1)
        pick_ref[...] = (iota((slots, rows), 0) == place).astype(F32).astype(BF16)

    lane = iota((rows, LANES), 1)
    low = lane < 64
    even = (lane & 32) == 0
    odd_row = (iota((rows // 8, 8, LANES), 1) & 1) == 1
    pick = pick_ref[...]
    for quad in range(quads):
        white = []
        for part in range(4):
            x = raw_ref[quad * 4 + part].astype(F32)
            square = (x * x).reshape(rows // 8, 8, LANES)
            other = jnp.where(odd_row, pltpu.roll(square, 1, 1), pltpu.roll(square, 7, 1))
            power = (square + other).reshape(rows, LANES)
            level = jnp.sum(power, axis=1, keepdims=True) * (1.0 / LANES)
            white.append(x * lax.rsqrt(power + level + 1e-05))
        w0, w1, w2, w3 = white
        a0 = jnp.where(low, w0, pltpu.roll(w2, 64, 1))
        a2 = jnp.where(low, pltpu.roll(w0, 64, 1), w2)
        a1 = jnp.where(low, w1, pltpu.roll(w3, 64, 1))
        a3 = jnp.where(low, pltpu.roll(w1, 64, 1), w3)
        d0 = jnp.where(even, a0, pltpu.roll(a1, 32, 1))
        d1 = jnp.where(even, pltpu.roll(a0, 96, 1), a1)
        d2 = jnp.where(even, a2, pltpu.roll(a3, 32, 1))
        d3 = jnp.where(even, pltpu.roll(a2, 96, 1), a3)
        for half, (first, second) in enumerate(((d0, d1), (d2, d3))):
            both = jnp.concatenate([first.astype(BF16), second.astype(BF16)], axis=1)
            sent = jnp.dot(pick, both, preferred_element_type=F32).astype(BF16)
            out_ref[2 * half, quad] = sent[:, :LANES]
            out_ref[2 * half + 1, quad] = sent[:, LANES:]


def whiten(raw, table, me):
    segments, rows, _ = raw.shape
    quads = segments // 4
    step = 3
    slots = table.shape[0] * MOST * 2
    return pl.pallas_call(
        functools.partial(whiten_kernel, me, step),
        out_shape=jax.ShapeDtypeStruct((4, quads, slots, LANES), BF16),
        grid=(quads // step,),
        in_specs=[
            pl.BlockSpec((4 * step, rows, LANES), lambda i: (i, 0, 0)),
            pl.BlockSpec(table.shape, lambda i: (0, 0)),
        ],
        out_specs=pl.BlockSpec((4, step, slots, LANES), lambda i: (0, i, 0, 0)),
        scratch_shapes=[pltpu.VMEM((slots, rows), BF16)],
        name="whiten",
    )(raw, table)


def build_pick(me, table_ref, pick_ref):
    slots = pick_ref.shape[0]
    shards, stations = table_ref.shape
    mine = jnp.sum((table_ref[...] == me).astype(F32), axis=1, keepdims=True)
    mine = jnp.broadcast_to(mine, (shards, LANES)).astype(BF16)
    lower = (iota((shards, shards), 1) < iota((shards, shards), 0)).astype(F32).astype(BF16)
    first = jnp.dot(lower, mine, preferred_element_type=F32)
    shard = iota((slots, shards), 1)
    row = iota((slots, shards), 0)
    member = ((row >= 6 * shard) & (row < 6 * shard + 6)).astype(F32).astype(BF16)
    first = jnp.dot(member, first.astype(BF16), preferred_element_type=F32)
    mine = jnp.dot(member, mine, preferred_element_type=F32)
    index = iota((shards, LANES), 0).astype(F32).astype(BF16)
    index = jnp.dot(member, index, preferred_element_type=F32)
    rest = iota((slots, LANES), 0).astype(F32) - 6.0 * index
    imag = (iota((slots, LANES), 0) & 1) == 1
    rank = 0.5 * (rest - jnp.where(imag, 1.0, 0.0))
    hit = (rank < mine) & (first + rank == iota((slots, LANES), 1).astype(F32))
    for part in range(2):
        chosen = jnp.where(hit & (imag == (part == 1)), 1.0, 0.0).astype(BF16)
        pick_ref[:, part * LANES:(part + 1) * LANES] = chosen


def gather_kernel(dims, relayed, parts, send, table, own, near, recv, relay, fresh, wide, pick,
                  send_sem, recv_sem, relay_sem, pass_sem, local_sem, send_far, recv_far, send_near, recv_near):
    days, ny, nz = dims
    blocks = ny * nz * 2
    quads = recv.shape[1]
    bins = fresh.shape[1]
    g = lax.axis_index("day")
    s = lax.axis_index("sta")
    y = lax.div(s, 2 * nz)
    z = lax.rem(lax.div(s, 2), nz)
    c = lax.rem(s, 2)
    owners = [lax.rem(g + turn, days) for turn in range(days)]
    partner = s + 1 - 2 * c

    def at(dy, dz, dc):
        return lax.rem(y + dy, ny) * (2 * nz) + lax.rem(z + dz, nz) * 2 + lax.rem(c + dc, 2)

    barrier = pltpu.get_barrier_semaphore()

    def greet(t, carry):
        peer = lax.rem(s + t, blocks)
        for d in owners:
            pl.semaphore_signal(barrier, inc=1, device_id=(d, peer), device_id_type=MESH)
        return carry

    lax.fori_loop(1, blocks, greet, 0)
    for d in owners[1:]:
        pl.semaphore_signal(barrier, inc=1, device_id=(d, s), device_id_type=MESH)
    pl.semaphore_wait(barrier, days * blocks - 1)

    spans = [pl.ds(first, count) for first, count in parts]

    def post(i, d, kind, block, target, dst, sem):
        pltpu.make_async_remote_copy(
            src_ref=send.at[d, spans[i], block], dst_ref=dst, send_sem=send_sem.at[2 * i + kind], recv_sem=sem,
            device_id=(d, target), device_id_type=MESH).start()

    def post_all(i, block, target, dst, sem, turns):
        for turn in turns:
            post(i, owners[turn], min(turn, 1), block, target, dst, sem)

    def post_half(i):
        def step(t, carry):
            block = at(lax.div(t, 2), nz // 2, lax.rem(t, 2))
            target = at(lax.div(t, 2), nz // 2 - 1, lax.rem(t, 2)) if relayed else block
            dst = relay.at[g, spans[i], y, c] if relayed else recv.at[g, spans[i], y, z, c]
            post_all(i, block, target, dst, relay_sem.at[i] if relayed else recv_sem.at[i], range(days))
            return carry

        lax.fori_loop(0, 2 * ny, step, 0)

    def post_rest(i):
        dst = recv.at[g, spans[i], y, z, c]

        def step(u, carry):
            k = lax.div(u, 2 * ny) + 1
            t = lax.rem(u, 2 * ny) + 2
            dz = lax.rem(nz + nz // 2 + lax.div(k + 1, 2) * (1 - 2 * lax.rem(k, 2)), nz)
            block = at(lax.div(t, 2), dz, lax.rem(t, 2) + 1)
            post_all(i, block, block, dst, recv_sem.at[i], range(days))
            return carry

        lax.fori_loop(0, 2 * ny * (nz - 1) - 1, step, 0)
        post_all(i, s, s, dst, recv_sem.at[i], range(1, days))

    def keep(i):
        pltpu.make_async_copy(send.at[g, spans[i], s], recv.at[g, spans[i], y, z, c], recv_sem.at[i]).start()

    def hand_on(i):
        return pltpu.make_async_remote_copy(
            src_ref=relay.at[:, spans[i]], dst_ref=recv.at[:, spans[i], :, lax.rem(z + nz // 2 + 1, nz)],
            send_sem=pass_sem.at[i], recv_sem=recv_sem.at[i], device_id=(g, at(0, 1, 0)), device_id_type=MESH)

    def await_relay(i):
        held = relay.at[:, spans[i]]
        pltpu.make_async_copy(held, held, relay_sem.at[i]).wait()

    def far(j):
        return pltpu.make_async_remote_copy(
            src_ref=own.at[j], dst_ref=near.at[1, j], send_sem=send_far.at[j], recv_sem=recv_far.at[j],
            device_id=(g, lax.rem(s + blocks - 2, blocks)), device_id_type=MESH)

    def close(j, source):
        return pltpu.make_async_remote_copy(
            src_ref=source.at[j], dst_ref=near.at[0, j], send_sem=send_near.at[j], recv_sem=recv_near.at[j],
            device_id=(g, partner), device_id_type=MESH)

    dense = recv.reshape(days, quads, blocks * MOST * 2, LANES)

    def arrange(i):
        held = recv.at[:, spans[i]]
        pltpu.make_async_copy(held, held, recv_sem.at[i]).wait()
        first, count = parts[i]
        for j in range(first, first + count):
            for day in range(days):
                block = lax.dot_general(dense[day, j], pick[...], (((0,), (0,)), ((), ())), preferred_element_type=F32)
                for part in range(4):
                    for kind in range(2):
                        where = pl.ds(kind * 4 * days + day * 4 + part, bins, stride=8 * days)
                        wide[where, :] = block[part * bins:(part + 1) * bins, kind * LANES:(kind + 1) * LANES]
            fresh[j] = wide[...].reshape(bins, 8 * days, LANES).astype(BF16)
            pltpu.make_async_copy(fresh.at[j], own.at[j], local_sem.at[j]).start()
        for j in range(first, first + count):
            pltpu.make_async_copy(fresh.at[j], own.at[j], local_sem.at[j]).wait()
            far(j).start()

    n = len(parts)
    if relayed:
        post_half(0)
        post_rest(0)
        keep(0)
        for i in range(1, n):
            post_half(i)
            await_relay(i - 1)
            hand_on(i - 1).start()
            post_rest(i)
            keep(i)
            if i == 1:
                build_pick(s, table, pick)
        for i in range(n):
            if i == 1 or n == 1:
                await_relay(n - 1)
                hand_on(n - 1).start()
            arrange(i)
    else:
        for i in range(n):
            post_half(i)
            post_rest(i)
            keep(i)
        build_pick(s, table, pick)
        for i in range(n):
            arrange(i)

    @pl.when(c == 1)
    def _():
        for j in range(quads):
            close(j, own).start()
        for j in range(quads):
            far(j).wait_recv()

    @pl.when(c == 0)
    def _():
        for j in range(quads):
            far(j).wait_recv()
            close(j, near.at[1]).start()

    for j in range(quads):
        close(j, own).wait_recv()
    for i in range(n):
        few = send.at[0, spans[i], pl.ds(0, blocks - 1)]
        pltpu.make_async_copy(few, few, send_sem.at[2 * i]).wait()
        rest = send.at[pl.ds(0, days - 1), spans[i]]
        pltpu.make_async_copy(rest, rest, send_sem.at[2 * i + 1]).wait()
        if relayed:
            hand_on(i).wait_send()
    for j in range(quads):
        close(j, own).wait_send()
        far(j).wait_send()


def gather(send, table, dims, relayed, parts):
    days, ny, nz = dims
    quads, blocks = send.shape[1:3]
    bins = LANES // 4
    n = len(parts)
    tail = (MOST, 2, LANES)
    piece = (quads, bins, 8 * days, LANES)
    dma = pltpu.SemaphoreType.DMA
    return pl.pallas_call(
        functools.partial(gather_kernel, dims, relayed, parts),
        out_shape=(jax.ShapeDtypeStruct(piece, BF16), jax.ShapeDtypeStruct((2,) + piece, BF16)),
        in_specs=[pl.BlockSpec(memory_space=pl.ANY), pl.BlockSpec(memory_space=pltpu.VMEM)],
        out_specs=(pl.BlockSpec(memory_space=pl.ANY), pl.BlockSpec(memory_space=pl.ANY)),
        scratch_shapes=[
            pltpu.VMEM((days, quads, ny, nz, 2) + tail, BF16),
            pltpu.VMEM((days, quads, ny, 2) + tail, BF16),
            pltpu.VMEM(piece, BF16),
            pltpu.VMEM((bins * 8 * days, LANES), F32),
            pltpu.VMEM((blocks * MOST * 2, 2 * LANES), BF16),
            dma((2 * n,)), dma((n,)), dma((n,)), dma((n,)), dma((quads,)),
            dma((quads,)), dma((quads,)), dma((quads,)), dma((quads,)),
        ],
        compiler_params=pltpu.CompilerParams(collective_id=0, has_side_effects=True),
        name="gather",
    )(send, table)


def correlate_kernel(scale, listed_ref, own_ref, near_ref, out_ref):
    quads, bins, depth, width = own_ref.shape
    half = depth // 2
    gains = [listed_ref[0, o].astype(F32) * scale for o in range(3)]
    for f in range(bins):
        own = [own_ref[j, f] for j in range(quads)]
        left = []
        for piece in own:
            real, imag = piece[:half], piece[half:]
            left.append(jnp.concatenate([real, -imag], axis=1))
            left.append(jnp.concatenate([imag, real], axis=1))
        right = [jnp.concatenate(own, axis=0)]
        for o in range(2):
            right.append(jnp.concatenate([near_ref[o, j, f] for j in range(quads)], axis=0))
        product = lax.dot_general(
            jnp.concatenate(left, axis=0), jnp.concatenate(right, axis=1), (((0,), (0,)), ((), ())),
            preferred_element_type=F32)
        for o in range(3):
            for part in range(2):
                piece = product[part * width:(part + 1) * width, o * width:(o + 1) * width]
                out_ref[0, o, part, f] = (piece * gains[o]).astype(BF16)


def stack(own, near, listed, scale):
    quads, bins, depth, width = own.shape
    step = 4
    return pl.pallas_call(
        functools.partial(correlate_kernel, scale),
        out_shape=jax.ShapeDtypeStruct((1, 3, 2, bins, width, width), BF16),
        grid=(bins // step,),
        in_specs=[
            pl.BlockSpec(memory_space=pltpu.SMEM),
            pl.BlockSpec((quads, step, depth, width), lambda i: (0, i, 0, 0)),
            pl.BlockSpec((2, quads, step, depth, width), lambda i: (0, 0, i, 0, 0)),
        ],
        out_specs=pl.BlockSpec((1, 3, 2, step, width, width), lambda i: (0, 0, 0, i, 0, 0)),
        name="stack",
    )(listed, own, near)


RELAYED = True
PARTS = ((0, 3), (3, 2), (5, 1))


def local(raw_spectra, station_block, pair_listed):
    blocks = lax.axis_size("sta")
    days = lax.axis_size("day")
    segments, stations, _, bins = raw_spectra.shape
    quads = segments // 4
    me = lambda: lax.axis_index("sta")
    table = station_block.reshape(blocks, stations)
    sent = whiten(raw_spectra.reshape(segments, 2 * stations, bins), table, me)
    sent = sent.reshape(days, quads, blocks, MOST, 2, LANES)
    own, near = gather(sent, table, (days, blocks // 16, 8), RELAYED, PARTS)
    scale = 1.0 / float(segments * days) ** 0.5
    return stack(own, near, pair_listed, scale)


def solution(mesh):
    in_specs = (P("day", "sta", None, None), P(), P("sta", None))
    out_specs = P("sta", None, None, "day", None, None)
    return jax.shard_map(local, mesh=mesh, in_specs=in_specs, out_specs=out_specs, check_vma=False)
```
